32 devices in a mesh: dp: 16 (over z, y, x), mp: 2 (over core).
Axes of the slice: x: 2, y: 2, z: 4, core: 2. Of those that a mesh axis runs over, the one named last changes fastest.
Arguments:
- inputs: bfloat16 [6144, 768], P('dp')
- cotangent: bfloat16 [6144, 768], P('dp'), may hold values from -6 to 6
- lengths: int32 [16, 3], P('dp'), may hold values from 0 to 192, as said below
- masked: int32 [6144], P('dp'), may hold values 0 or 1
- replace_ids: int32 [6144], P('dp'), may hold values from 0 to 15359, as said below
- attention_master: float32 [4, 768, 768], P(None, 'dp', 'mp')
- attention_moment: float32 [4, 768, 768], P(None, 'dp', 'mp'), may hold values from -0.1875 to 0.1875
- attention_square: float32 [4, 768, 768], P(None, 'dp', 'mp'), may hold values from 0.00016276042 to 0.0006510417
- geglu_master: float32 [3, 768, 3072], P(None, 'dp', 'mp')
- geglu_moment: float32 [3, 768, 3072], P(None, 'dp', 'mp'), may hold values from -0.1875 to 0.1875
- geglu_square: float32 [3, 768, 3072], P(None, 'dp', 'mp'), may hold values from 0.00016276042 to 0.0006510417
- embed_master: float32 [15360, 768], P('dp', 'mp'), may hold values from -6 to 6
- embed_moment: float32 [15360, 768], P('dp', 'mp'), may hold values from -0.0008544922 to 0.0008544922
- embed_square: float32 [15360, 768], P('dp', 'mp'), may hold values from 3.1789145e-09 to 1.2715658e-08
- norms_master: float32 [4, 768], replicated
- norms_moment: float32 [4, 768], replicated, may hold values from -0.1875 to 0.1875
- norms_square: float32 [4, 768], replicated, may hold values from 0.00016276042 to 0.0006510417
Outputs:
- output: float32 [6144, 768], P('dp')
- input_grad: float32 [6144, 768], P('dp')
- rms_stats: float32 [3], replicated
- lamb_norms: float32 [2, 12], replicated
- attention_grad: float32 [4, 768, 768], P(None, 'dp', 'mp')
- attention_first: float32 [4, 768, 768], P(None, 'dp', 'mp')
- attention_second: float32 [4, 768, 768], P(None, 'dp', 'mp')
- attention_new: float32 [4, 768, 768], P(None, 'dp', 'mp')
- geglu_grad: float32 [3, 768, 3072], P(None, 'dp', 'mp')
- geglu_first: float32 [3, 768, 3072], P(None, 'dp', 'mp')
- geglu_second: float32 [3, 768, 3072], P(None, 'dp', 'mp')
- geglu_new: float32 [3, 768, 3072], P(None, 'dp', 'mp')
- embed_grad: float32 [15360, 768], P('dp', 'mp')
- embed_first: float32 [15360, 768], P('dp', 'mp')
- embed_second: float32 [15360, 768], P('dp', 'mp')
- embed_new: float32 [15360, 768], P('dp', 'mp')
- norms_grad: float32 [4, 768], replicated
- norms_first: float32 [4, 768], replicated
- norms_second: float32 [4, 768], replicated
- norms_new: float32 [4, 768], replicated
The draws below stay inside these ranges and needn't reach their ends.
Inputs may be any that keep to these rules, and one draw needn't show every extreme that they name: Row d lists the lengths of the sequences given to device d, zeros after; each sequence has 128 tokens or more; a row sums to at most 384, and some row reaches it with a sequence of 192. `replace_ids`: among the 384 slots of one device, exactly 24 ids fall in each aligned block of 960 table rows.
All inputs are finite; a program needn't handle non-finite values. No bound on the sum of `masked` on one device may be relied on, other than what follows from the above.
Results may differ from the reference program's by a relative error of at most 0.016.
The reference program's roundings to bfloat16 on the way count: a program that leaves them out, or rounds other values in their place, can miss the bound.
Values may be sent and summed in bfloat16 or wider, within the bound.
A program may use at most 192 MiB of HBM per device.

```python
import math
import jax
import jax.numpy as jnp
from jax import lax

D = 768
HEADS = 12
FF = 3072
HEAD_DIM = 64
VOCAB = 15360
TOK_DEV = 384
MINLEN = 128
STEP_COUNT = 6
MAXLEN = 192
MINTOK = 128
TOKENS = 6144
N_DP = 16


def draw_inputs(key, part):
    row_count = N_DP * TOK_DEV
    device_pos = (jnp.arange(row_count) // TOK_DEV).astype(jnp.float32)
    row_scale = 0.6 * 3.0 ** (device_pos / max(N_DP - 1, 1))
    noise = jax.random.normal(key, (row_count, D), jnp.float32)
    return (noise * row_scale[:, None]).astype(jnp.bfloat16)


def draw_replace_ids(key, part):
    per_owner = TOK_DEV // N_DP
    owner_rows = VOCAB // N_DP
    device_keys = jax.random.split(jax.random.fold_in(key, 11), N_DP)
    shuffled = jax.vmap(lambda one_key: jax.random.permutation(one_key, TOK_DEV))(device_keys)
    owner = shuffled // per_owner
    offset = jax.random.randint(jax.random.fold_in(key, 12), (N_DP, TOK_DEV), 0, owner_rows)
    return (owner * owner_rows + offset).reshape(N_DP * TOK_DEV).astype(jnp.int32)


def draw_attention_master(key, part):
    noise = jax.random.normal(key, (4, D, D), jnp.float32)
    factor = jnp.where(jnp.arange(4) < 3, D ** (-0.5), (D // 8) ** (-0.5))
    return noise * factor[:, None, None]


def draw_geglu_master(key, part):
    noise = jax.random.normal(key, (3, D, FF), jnp.float32)
    factor = jnp.where(jnp.arange(3) < 2, D ** (-0.5), 1.5 * FF ** (-0.5))
    return noise * factor[:, None, None]


def draw_norms_master(key, part):
    noise = jax.random.normal(key, (4, D), jnp.float32)
    centre = jnp.where(jnp.arange(4) % 2 == 0, 1.0, 0.0)
    return centre[:, None] + 0.1 * noise


def draw_lengths(key, part):
    key_one, key_two, key_three, key_four = jax.random.split(key, 4)
    slot_count = TOK_DEV // MINLEN
    budget = jax.random.randint(key_one, (N_DP, 1), MINTOK, TOK_DEV + 1)
    opener = jax.random.randint(key_two, (N_DP, 1), MINLEN, jnp.minimum(MAXLEN, budget) + 1)
    later = jax.random.randint(key_three, (N_DP, slot_count - 1), MINLEN, MAXLEN + 1)
    running = opener + jnp.cumsum(later, axis=1)
    kept = running <= budget
    later = jnp.where(kept, later, 0)
    kept_count = jnp.sum(kept.astype(jnp.int32), axis=1, keepdims=True)
    leftover = budget - opener - jnp.sum(later, axis=1, keepdims=True)
    slot_pos = jnp.arange(slot_count - 1)[None, :]
    later = later + jnp.where((slot_pos == kept_count) & (leftover >= MINLEN), leftover, 0)
    drawn_table = jnp.concatenate([opener, later], axis=1)
    forced_dev = jax.random.randint(key_four, (), 0, N_DP)
    positions = jnp.arange(slot_count)
    copies = TOK_DEV // MAXLEN
    forced_row = jnp.where(positions < copies, MAXLEN, jnp.where(positions == copies, TOK_DEV % MAXLEN, 0))
    chosen = jnp.arange(N_DP)[:, None] == forced_dev
    return jnp.where(chosen, forced_row[None, :], drawn_table).astype(jnp.int32)


def with_ends(drawn, rng, least, top_value):
    index_at = [jax.random.randint(jax.random.fold_in(rng, axis), (), 0, length) for axis, length in enumerate(drawn.shape)]
    widest = drawn.shape.index(max(drawn.shape))
    neighbour = index_at[:widest] + [(index_at[widest] + 1) % drawn.shape[widest]] + index_at[widest + 1:]
    return drawn.at[tuple(index_at)].set(least).at[tuple(neighbour)].set(top_value)


def steps_of(stream_key, shape, pieces, least, high):
    factor_of = 1.0
    for axis_at, parts in pieces:
        heights = jax.random.uniform(jax.random.fold_in(jax.random.fold_in(stream_key, 6), axis_at), (parts,), jnp.float32, least / len(pieces), high / len(pieces))
        factor_of = factor_of * jnp.repeat(jnp.exp(heights), shape[axis_at] // parts).reshape((-1,) + (1,) * (len(shape) - 1 - axis_at))
    return factor_of


def centred(key, shape, width, most, cuts=(), held_as=jnp.bfloat16):
    drawn = jax.random.normal(key, shape, jnp.float32) * width
    if len(cuts) > 0:
        drawn = steps_of(key, shape, cuts, -0.22, 0.18) * drawn
    return jnp.clip(drawn, min=-most, max=most).astype(held_as)


def setup_inputs(seed: int = 0) -> dict:
    keys = jax.random.split(jax.random.key(seed), 18)
    return {
        "inputs": draw_inputs(jax.random.fold_in(keys[17], 71), 0),
        "cotangent": centred(keys[1], (TOKENS, D), 1.0, 6.0, ((0, 16),)),
        "lengths": draw_lengths(jax.random.fold_in(keys[17], 71), 0),
        "masked": with_ends((jax.random.randint(keys[3], (TOKENS,), 0, 10) < 3).astype(jnp.int32), jax.random.fold_in(keys[3], 1), 0, 1),
        "replace_ids": draw_replace_ids(jax.random.fold_in(keys[17], 71), 0),
        "attention_master": draw_attention_master(jax.random.fold_in(keys[17], 71), 0),
        "attention_moment": centred(keys[6], (4, D, D), ((TOK_DEV * N_DP) ** -0.5), 0.1875, ((1, 16), (2, 2)), jnp.float32),
        "attention_square": jnp.clip(jnp.exp(math.log(0.0006510417) - 1.3862944 * jax.random.uniform(keys[7], (4, D, D), jnp.float32) ** steps_of(keys[7], (4, D, D), ((1, 16), (2, 2)), -0.2, 0.2)), 0.00016276042, 0.0006510417),
        "geglu_master": draw_geglu_master(jax.random.fold_in(keys[17], 71), 0),
        "geglu_moment": centred(keys[9], (3, D, FF), ((TOK_DEV * N_DP) ** -0.5), 0.1875, ((1, 16), (2, 2)), jnp.float32),
        "geglu_square": jnp.clip(jnp.exp(math.log(0.0006510417) - 1.3862944 * jax.random.uniform(keys[10], (3, D, FF), jnp.float32) ** steps_of(keys[10], (3, D, FF), ((1, 16), (2, 2)), -0.2, 0.2)), 0.00016276042, 0.0006510417),
        "embed_master": centred(keys[11], (VOCAB, D), 1.0, 6.0, ((0, 16), (1, 2)), jnp.float32),
        "embed_moment": centred(keys[12], (VOCAB, D), ((3 * (10 * VOCAB * TOK_DEV * N_DP) ** -1) ** 0.5), 0.0008544922, ((0, 16), (1, 2)), jnp.float32),
        "embed_square": jnp.clip(jnp.exp(math.log(1.2715657859985185e-08) - 1.3862944 * jax.random.uniform(keys[13], (VOCAB, D), jnp.float32) ** steps_of(keys[13], (VOCAB, D), ((0, 16), (1, 2)), -0.2, 0.2)), 3.1789144649962964e-09, 1.2715657859985185e-08),
        "norms_master": draw_norms_master(jax.random.fold_in(keys[17], 71), 0),
        "norms_moment": centred(keys[15], (4, D), ((TOK_DEV * N_DP) ** -0.5), 0.1875, (), jnp.float32),
        "norms_square": jnp.clip(jnp.exp(jax.random.uniform(keys[16], (4, D), jnp.float32, math.log(0.00016276042), math.log(0.0006510417))), 0.00016276042, 0.0006510417),
    }


@jax.custom_vjp
def low(v):
    return lax.optimization_barrier(v.astype(jnp.bfloat16)).astype(jnp.float32)

@jax.custom_vjp
def low_back(v):
    return v

def low_keep(v):
    return (low(v), None)

def low_pass(kept, grad):
    return (grad,)

def back_keep(v):
    return (v, None)

def back_low(kept, grad):
    return (low(grad),)
low.defvjp(low_keep, low_pass)
low_back.defvjp(back_keep, back_low)
first_decay = 0.5
second_decay = 0.5
learn_rate = 0.3
matrix_decay = 0.01
adam_epsilon = 1e-06
norm_epsilon = 1e-12
masked_score = -1000000000.0
highest = lax.Precision.HIGHEST

def layer_norm(values, gain_row, shift_row):
    center = values - lax.optimization_barrier(jnp.mean(values, axis=-1, keepdims=True))
    spread = lax.optimization_barrier(jnp.mean(center * center, axis=-1, keepdims=True))
    return center * lax.rsqrt(spread + norm_epsilon) * gain_row + shift_row

def segment_of(length_row):
    ends_at = jnp.cumsum(length_row).astype(jnp.int32)
    places = jnp.arange(TOK_DEV, dtype=jnp.int32)
    return lax.optimization_barrier(jnp.sum((ends_at[None, :] <= places[:, None]).astype(jnp.int32), axis=1))

def attend(queries, keys_all, values_all, segment_ids):
    block_len = min(TOK_DEV, 512)
    places = jnp.arange(TOK_DEV, dtype=jnp.int32)
    slopes = 2.0 ** (-8.0 * (jnp.arange(HEADS, dtype=jnp.float32) + 1.0) / HEADS)
    attn_scale = 1.0 / math.sqrt(HEAD_DIM)

    def one_block(begin_at):
        query_blk = lax.dynamic_slice_in_dim(queries, begin_at, block_len, 0)
        query_pos = begin_at + jnp.arange(block_len, dtype=jnp.int32)
        query_seg = lax.dynamic_slice_in_dim(segment_ids, begin_at, block_len, 0)
        scores = jnp.einsum('qhe,khe->hqk', query_blk, keys_all, precision=highest) * attn_scale
        distance = jnp.abs(query_pos[:, None] - places[None, :]).astype(jnp.float32)
        scores = scores - slopes[:, None, None] * distance[None]
        same_seq = query_seg[:, None] == segment_ids[None, :]
        scores = low_back(jnp.where(same_seq[None], scores, masked_score))
        weights = low(jax.nn.softmax(scores, axis=-1))
        return jnp.einsum('hqk,khe->qhe', weights, values_all, precision=highest)
    starts = jnp.arange(TOK_DEV // block_len, dtype=jnp.int32) * block_len
    context = lax.map(jax.checkpoint(one_block), starts)
    return context.reshape(TOK_DEV, HEADS * HEAD_DIM)

def device_pass(attn_low, geglu_low, table_low, norm_params, hidden_dev, masked_dev, ids_dev, length_row):
    looked = jnp.take(table_low, ids_dev, axis=0)
    hidden_in = jnp.where(masked_dev[:, None] == 1, looked, hidden_dev)
    segment_ids = segment_of(length_row)
    act_low = low(hidden_in)
    qkv_all = jnp.einsum('td,kdc->ktc', act_low, attn_low[:3], precision=highest)
    qkv_all = low_back(low(qkv_all)).reshape(3, TOK_DEV, HEADS, HEAD_DIM)
    context = attend(qkv_all[0], qkv_all[1], qkv_all[2], segment_ids)
    context = low_back(low(context))
    attn_out = low_back(jnp.einsum('tc,dc->td', context, attn_low[3], precision=highest))
    normed_one = layer_norm(hidden_in + attn_out, norm_params[0], norm_params[1])
    gate_up = low_back(jnp.einsum('td,kdf->ktf', low(normed_one), geglu_low[:2], precision=highest))
    inner_act = low(jax.nn.gelu(gate_up[0], approximate=True) * gate_up[1])
    geglu_out = low_back(jnp.einsum('tf,df->td', inner_act, geglu_low[2], precision=highest))
    result = layer_norm(normed_one + geglu_out, norm_params[2], norm_params[3])
    live_rows = (jnp.arange(TOK_DEV) < jnp.sum(length_row)).astype(jnp.float32)[:, None]
    squares = jnp.stack([jnp.sum(hidden_in * hidden_in * live_rows), jnp.sum(attn_out * attn_out * live_rows), jnp.sum(geglu_out * geglu_out * live_rows)])
    return (result, squares)

def lamb_step(master, moment, square, gradient, decay_rate, sum_axes):
    new_moment = first_decay * moment + (1.0 - first_decay) * gradient
    new_square = second_decay * square + (1.0 - second_decay) * gradient * gradient
    update = new_moment / (1.0 - first_decay ** STEP_COUNT) / (jnp.sqrt(new_square / (1.0 - second_decay ** STEP_COUNT)) + adam_epsilon) + decay_rate * master
    weight_norm = jnp.sqrt(lax.optimization_barrier(jnp.sum(master * master, axis=sum_axes, keepdims=True)))
    update_norm = jnp.sqrt(lax.optimization_barrier(jnp.sum(update * update, axis=sum_axes, keepdims=True)))
    new_master = master - learn_rate * (weight_norm / update_norm) * update
    return (new_moment, new_square, new_master, weight_norm.reshape(-1), update_norm.reshape(-1))

def reference(inputs, cotangent, lengths, masked, replace_ids, attention_master, attention_moment, attention_square, geglu_master, geglu_moment, geglu_square, embed_master, embed_moment, embed_square, norms_master, norms_moment, norms_square):

    def forward(attn_master, mlp_master, table_master, norm_params, hidden):
        attn_low = low(attn_master)
        geglu_low = low(mlp_master)
        table_low = low(table_master)

        def one_device(packed):
            return device_pass(attn_low, geglu_low, table_low, norm_params, packed[0], packed[1], packed[2], packed[3])
        packed_all = (hidden.reshape(N_DP, TOK_DEV, D), masked.reshape(N_DP, TOK_DEV), replace_ids.reshape(N_DP, TOK_DEV), lengths)
        results, squares = lax.map(jax.checkpoint(one_device), packed_all)
        return (results.reshape(N_DP * TOK_DEV, D), squares)
    result, pull_back, squares = jax.vjp(forward, attention_master, geglu_master, embed_master, norms_master, inputs.astype(jnp.float32), has_aux=True)
    live_rows = (jnp.arange(TOK_DEV)[None, :] < lax.optimization_barrier(jnp.sum(lengths, axis=1))[:, None]).astype(jnp.float32).reshape(N_DP * TOK_DEV, 1)
    attn_sum, mlp_sum, table_sum, norm_sum, input_grad = pull_back(cotangent.astype(jnp.float32) * live_rows)
    token_total = jnp.sum(lengths).astype(jnp.float32)
    rms_stats = jnp.sqrt(lax.optimization_barrier(jnp.sum(squares, axis=0)) / (token_total * D) + 1e-06)
    attn_grad = attn_sum / token_total
    mlp_grad = mlp_sum / token_total
    table_grad = table_sum / token_total
    norm_grad = norm_sum / token_total
    attn_parts = lamb_step(attention_master, attention_moment, attention_square, attn_grad, matrix_decay, (1, 2))
    mlp_parts = lamb_step(geglu_master, geglu_moment, geglu_square, mlp_grad, matrix_decay, (1, 2))
    table_parts = lamb_step(embed_master, embed_moment, embed_square, table_grad, matrix_decay, (0, 1))
    norm_parts = lamb_step(norms_master, norms_moment, norms_square, norm_grad, 0.0, (1,))
    lamb_norms = jnp.stack([jnp.concatenate([attn_parts[3], mlp_parts[3], table_parts[3], norm_parts[3]]), jnp.concatenate([attn_parts[4], mlp_parts[4], table_parts[4], norm_parts[4]])])
    return (result, input_grad, rms_stats, lamb_norms, attn_grad, attn_parts[0], attn_parts[1], attn_parts[2], mlp_grad, mlp_parts[0], mlp_parts[1], mlp_parts[2], table_grad, table_parts[0], table_parts[1], table_parts[2], norm_grad, norm_parts[0], norm_parts[1], norm_parts[2])
```

```python
import math

import jax
import jax.numpy as jnp
from jax import lax
from jax.sharding import PartitionSpec as P

HEADS = 12
STEP_COUNT = 6


first_decay = 0.5
second_decay = 0.5
learn_rate = 0.3
matrix_decay = 0.01
adam_epsilon = 1e-06
norm_epsilon = 1e-12
masked_score = -1000000000.0


def cut_along(value, dim, length):
    dims = value.shape
    tiles = value.reshape(*dims[:dim], length, dims[dim] // length, *dims[dim + 1 :])
    return jnp.moveaxis(tiles, dim, 0)


def sent_and_summed(value, axis, dim):
    length = lax.axis_size(axis)
    tiles = lax.all_to_all(cut_along(value, dim, length), axis, 0, 0, tiled=True)
    return jnp.sum(tiles.astype(jnp.float32), axis=0)


def layer_norm(values, gain_row, shift_row):
    center = values - jnp.mean(values, axis=-1, keepdims=True)
    spread = jnp.mean(center * center, axis=-1, keepdims=True)
    return center * lax.rsqrt(spread + norm_epsilon) * gain_row + shift_row


def norm_pair(values, gain_pair):
    return layer_norm(values, gain_pair[0], gain_pair[1])


def lamb_parts(master, moment, square, gradient, decay_rate):
    new_moment = first_decay * moment + (1.0 - first_decay) * gradient
    new_square = second_decay * square + (1.0 - second_decay) * gradient * gradient
    update = (
        new_moment
        / (1.0 - first_decay**STEP_COUNT)
        / (jnp.sqrt(new_square / (1.0 - second_decay**STEP_COUNT)) + adam_epsilon)
        + decay_rate * master
    )
    return (new_moment, new_square, update)


def gelu_tanh(values):
    return jax.nn.gelu(values, approximate=True)


def local(
    inputs,
    cotangent,
    lengths,
    masked,
    replace_ids,
    attention_master,
    attention_moment,
    attention_square,
    geglu_master,
    geglu_moment,
    geglu_square,
    embed_master,
    embed_moment,
    embed_square,
    norms_master,
    norms_moment,
    norms_square,
):
    half_type = jnp.bfloat16
    full_type = jnp.float32
    tokens_here = inputs.shape[0]
    width = inputs.shape[1]
    head_dim = width // HEADS
    local_heads = HEADS // lax.axis_size("mp")
    block_len = min(tokens_here, 512)
    attn_scale = 1.0 / math.sqrt(head_dim)
    column_count = embed_master.shape[1]
    attn_low, geglu_low = (
        lax.all_gather(attention_master.astype(half_type), "dp", axis=1, tiled=True),
        lax.all_gather(geglu_master.astype(half_type), "dp", axis=1, tiled=True),
    )
    owners = lax.axis_size("dp")
    owner_rows = embed_master.shape[0]
    per_owner = tokens_here // owners
    owner_low = jnp.arange(owners, dtype=jnp.int32)[:, None] * owner_rows
    owned = (replace_ids[None, :] >= owner_low) & (replace_ids[None, :] < owner_low + owner_rows)
    order = jnp.arange(tokens_here, dtype=jnp.int32)
    earlier = (order[:, None] < order[None, :]).astype(half_type)
    rank = jnp.dot(owned.astype(half_type), earlier, preferred_element_type=full_type)
    owner_at = jnp.arange(owners, dtype=full_type)[:, None] * per_owner
    target = jnp.sum(jnp.where(owned, rank + owner_at, 0.0), axis=0).astype(jnp.int32)
    moves = target[None, :] == order[:, None]
    sorted_ids = jnp.sum(jnp.where(moves, replace_ids[None, :], 0), axis=1)
    asked = lax.all_to_all(sorted_ids, "dp", 0, 0, tiled=True)
    asked = asked - lax.axis_index("dp") * owner_rows
    hits = asked[:, None] == jnp.arange(owner_rows, dtype=jnp.int32)[None, :]
    sent_rows = jnp.dot(
        hits.astype(half_type), embed_master.astype(half_type), preferred_element_type=full_type
    ).astype(half_type)
    got_rows = lax.all_to_all(sent_rows, "dp", 0, 0, tiled=True)
    looked_cols = jnp.einsum(
        "pt,pc->tc", moves.astype(half_type), got_rows, preferred_element_type=full_type
    ).astype(half_type)
    looked = lax.all_gather(looked_cols, "mp", axis=1, tiled=True)
    is_masked = masked[:, None] == 1
    hidden_in = jnp.where(is_masked, looked.astype(full_type), inputs.astype(full_type))
    length_row = lengths[0]
    places = jnp.arange(tokens_here, dtype=jnp.int32)
    ends_at = jnp.cumsum(length_row)
    segment_ids = jnp.sum((ends_at[None, :] <= places[:, None]).astype(jnp.int32), axis=1)
    live_rows = (places < jnp.sum(length_row)).astype(full_type)[:, None]
    token_count = jnp.sum(length_row).astype(full_type)
    head_ids = lax.axis_index("mp") * local_heads + jnp.arange(local_heads, dtype=jnp.int32)
    slopes = 2.0 ** (-8.0 * (head_ids.astype(full_type) + 1.0) / HEADS)
    act_low = hidden_in.astype(half_type)
    qkv_low = jnp.einsum(
        "td,kdc->ktc", act_low, attn_low[:3], preferred_element_type=full_type
    ).astype(half_type)
    head_vals = qkv_low.reshape(3, tokens_here, local_heads, head_dim)

    def block_scores(begin_at, query_blk):
        query_pos = begin_at + jnp.arange(block_len, dtype=jnp.int32)
        scores = (
            jnp.einsum("qhe,khe->hqk", query_blk, head_vals[1], preferred_element_type=full_type)
            * attn_scale
        )
        distance = jnp.abs(query_pos[:, None] - places[None, :]).astype(full_type)
        scores = scores - slopes[:, None, None] * distance[None]
        same_seq = segment_ids[:, None] == segment_ids[None, :]
        return jnp.where(same_seq[None], scores, masked_score)

    def forward_block(begin_at):
        query_blk = head_vals[0]
        scores = block_scores(begin_at, query_blk)
        top_score = jnp.max(scores, axis=-1, keepdims=True)
        raised = jnp.exp(scores - top_score)
        row_total = jnp.sum(raised, axis=-1, keepdims=True)
        weights = (raised / row_total).astype(half_type)
        context_blk = jnp.einsum(
            "hqk,khe->qhe", weights, head_vals[2], preferred_element_type=full_type
        )
        return (context_blk.astype(half_type), (top_score + jnp.log(row_total))[..., 0])

    starts = jnp.arange(tokens_here // block_len, dtype=jnp.int32) * block_len
    context_blocks, lse_blocks = lax.map(forward_block, starts)
    context = context_blocks.reshape(tokens_here, local_heads * head_dim)
    attn_part = jnp.einsum("tc,dc->td", context, attn_low[3], preferred_element_type=full_type)
    attn_out = lax.psum(attn_part, "mp")
    normed_one, first_back = jax.vjp(norm_pair, hidden_in + attn_out, norms_master[0:2])
    normed_low = normed_one.astype(half_type)
    gate_up = jnp.einsum("td,kdf->ktf", normed_low, geglu_low[:2], preferred_element_type=full_type)
    gelu_val, gelu_back = jax.vjp(gelu_tanh, gate_up[0])
    inner_act = (gelu_val * gate_up[1]).astype(half_type)
    geglu_part = jnp.einsum("tf,df->td", inner_act, geglu_low[2], preferred_element_type=full_type)
    geglu_out = lax.psum(geglu_part, "mp")
    result, second_back = jax.vjp(norm_pair, normed_one + geglu_out, norms_master[2:4])
    squares = jnp.stack(
        [
            jnp.sum(hidden_in * hidden_in * live_rows),
            jnp.sum(attn_out * attn_out * live_rows),
            jnp.sum(geglu_out * geglu_out * live_rows),
        ]
    )
    count_total, square_total = lax.psum((token_count, squares), "dp")
    rms_stats = jnp.sqrt(square_total / (count_total * width) + 1e-06)
    grad_second, norm_grad_two = second_back(cotangent.astype(full_type) * live_rows)
    grad_geglu = grad_second.astype(half_type)
    grad_inner = jnp.einsum("td,df->tf", grad_geglu, geglu_low[2], preferred_element_type=full_type)
    down_grad = jnp.einsum("td,tf->df", grad_geglu, inner_act, preferred_element_type=full_type)
    grad_gate = gelu_back(grad_inner * gate_up[1])[0]
    grad_up = grad_inner * gelu_val
    grad_gu = jnp.stack([grad_gate, grad_up]).astype(half_type)
    gu_grad = jnp.einsum("td,ktf->kdf", normed_low, grad_gu, preferred_element_type=full_type)
    geglu_local = jnp.concatenate([gu_grad, down_grad[None]], axis=0)
    back_part = jnp.einsum("ktf,kdf->td", grad_gu, geglu_low[:2], preferred_element_type=full_type)
    grad_normed = grad_second + lax.psum(back_part, "mp")
    grad_first_in, norm_grad_one = first_back(grad_normed)
    grad_attn = grad_first_in.astype(half_type)
    grad_context = jnp.einsum(
        "td,dc->tc", grad_attn, attn_low[3], preferred_element_type=full_type
    ).astype(half_type)
    out_grad = jnp.einsum("td,tc->dc", grad_attn, context, preferred_element_type=full_type)
    grad_heads = grad_context.reshape(tokens_here, local_heads, head_dim)

    def backward_block(carry, packed):
        key_acc, value_acc = carry
        begin_at, lse_blk = packed
        query_blk = head_vals[0]
        scores = block_scores(begin_at, query_blk)
        weights = jnp.exp(scores - lse_blk[..., None])
        grad_weights = jnp.einsum(
            "qhe,khe->hqk", grad_heads, head_vals[2], preferred_element_type=full_type
        )
        value_acc = value_acc + jnp.einsum(
            "hqk,qhe->khe", weights.astype(half_type), grad_heads, preferred_element_type=full_type
        )
        row_inner = jnp.sum(grad_weights * weights, axis=-1, keepdims=True)
        grad_scores = (weights * (grad_weights - row_inner)).astype(half_type)
        grad_query = (
            jnp.einsum("hqk,khe->qhe", grad_scores, head_vals[1], preferred_element_type=full_type)
            * attn_scale
        )
        key_acc = (
            key_acc
            + jnp.einsum("hqk,qhe->khe", grad_scores, query_blk, preferred_element_type=full_type)
            * attn_scale
        )
        return ((key_acc, value_acc), grad_query.astype(half_type))

    zero_heads = jnp.zeros((tokens_here, local_heads, head_dim), full_type)
    (key_acc, value_acc), query_grads = lax.scan(
        backward_block, (zero_heads, zero_heads), (starts, lse_blocks)
    )
    grad_qkv = jnp.stack(
        [
            query_grads.reshape(tokens_here, -1),
            key_acc.reshape(tokens_here, -1).astype(half_type),
            value_acc.reshape(tokens_here, -1).astype(half_type),
        ]
    )
    qkv_grad = jnp.einsum("td,ktc->kdc", act_low, grad_qkv, preferred_element_type=full_type)
    act_part = jnp.einsum("ktc,kdc->td", grad_qkv, attn_low[:3], preferred_element_type=full_type)
    grad_in = grad_first_in + lax.psum(act_part.astype(jnp.bfloat16), "mp").astype(jnp.float32)
    input_grad = jnp.where(is_masked, 0.0, grad_in)
    attention_local = jnp.concatenate([qkv_grad, out_grad[None]], axis=0)
    own_columns = lax.dynamic_slice_in_dim(
        grad_in, lax.axis_index("mp") * column_count, column_count, 1
    )
    picked = jnp.where(is_masked, own_columns, 0.0)
    highest = lax.Precision.HIGHEST
    sorted_grads = jnp.dot(moves.astype(full_type), picked, precision=highest)
    got_grads = lax.all_to_all(sorted_grads, "dp", 0, 0, tiled=True)
    embed_summed = jnp.einsum("pr,pc->rc", hits.astype(full_type), got_grads, precision=highest)
    attention_summed, geglu_summed = (
        sent_and_summed(attention_local.astype(jnp.bfloat16), "dp", 1),
        sent_and_summed(geglu_local.astype(jnp.bfloat16), "dp", 1),
    )
    inverse_count = 1.0 / count_total
    attention_grad = attention_summed * inverse_count
    geglu_grad = geglu_summed * inverse_count
    embed_grad = embed_summed * inverse_count
    attention_first, attention_second, attention_update = lamb_parts(
        attention_master, attention_moment, attention_square, attention_grad, matrix_decay
    )
    geglu_first, geglu_second, geglu_update = lamb_parts(
        geglu_master, geglu_moment, geglu_square, geglu_grad, matrix_decay
    )
    embed_first, embed_second, embed_update = lamb_parts(
        embed_master, embed_moment, embed_square, embed_grad, matrix_decay
    )
    weight_squares = jnp.concatenate(
        [
            jnp.sum(attention_master * attention_master, axis=(1, 2)),
            jnp.sum(geglu_master * geglu_master, axis=(1, 2)),
            jnp.sum(embed_master * embed_master)[None],
        ]
    )
    update_squares = jnp.concatenate(
        [
            jnp.sum(attention_update * attention_update, axis=(1, 2)),
            jnp.sum(geglu_update * geglu_update, axis=(1, 2)),
            jnp.sum(embed_update * embed_update)[None],
        ]
    )
    norms_local = jnp.concatenate([norm_grad_one, norm_grad_two], axis=0)
    weight_total, update_total, norms_summed = lax.psum(
        (weight_squares, update_squares, norms_local * 0.5), ("dp", "mp")
    )
    weight_norms = jnp.sqrt(weight_total)
    update_norms = jnp.sqrt(update_total)
    ratios = weight_norms / update_norms
    attention_new = attention_master - learn_rate * ratios[0:4][:, None, None] * attention_update
    geglu_new = geglu_master - learn_rate * ratios[4:7][:, None, None] * geglu_update
    embed_new = embed_master - learn_rate * ratios[7] * embed_update
    norms_grad = norms_summed * inverse_count
    norms_first, norms_second, norms_update = lamb_parts(
        norms_master, norms_moment, norms_square, norms_grad, 0.0
    )
    norm_weight = jnp.sqrt(jnp.sum(norms_master * norms_master, axis=1))
    norm_update = jnp.sqrt(jnp.sum(norms_update * norms_update, axis=1))
    norms_new = norms_master - learn_rate * (norm_weight / norm_update)[:, None] * norms_update
    lamb_norms = jnp.stack(
        [jnp.concatenate([weight_norms, norm_weight]), jnp.concatenate([update_norms, norm_update])]
    )
    return (
        result,
        input_grad,
        rms_stats,
        lamb_norms,
        attention_grad,
        attention_first,
        attention_second,
        attention_new,
        geglu_grad,
        geglu_first,
        geglu_second,
        geglu_new,
        embed_grad,
        embed_first,
        embed_second,
        embed_new,
        norms_grad,
        norms_first,
        norms_second,
        norms_new,
    )


def solution(mesh):
    in_specs = (
        P("dp", None),
        P("dp", None),
        P("dp", None),
        P("dp"),
        P("dp"),
        P(None, "dp", "mp"),
        P(None, "dp", "mp"),
        P(None, "dp", "mp"),
        P(None, "dp", "mp"),
        P(None, "dp", "mp"),
        P(None, "dp", "mp"),
        P("dp", "mp"),
        P("dp", "mp"),
        P("dp", "mp"),
        P(),
        P(),
        P(),
    )
    out_specs = (
        P("dp", None),
        P("dp", None),
        P(),
        P(),
        P(None, "dp", "mp"),
        P(None, "dp", "mp"),
        P(None, "dp", "mp"),
        P(None, "dp", "mp"),
        P(None, "dp", "mp"),
        P(None, "dp", "mp"),
        P(None, "dp", "mp"),
        P(None, "dp", "mp"),
        P("dp", "mp"),
        P("dp", "mp"),
        P("dp", "mp"),
        P("dp", "mp"),
        P(),
        P(),
        P(),
        P(),
    )
    return jax.shard_map(local, mesh=mesh, in_specs=in_specs, out_specs=out_specs, check_vma=False)
```

```python
import math

import jax
import jax.numpy as jnp
from jax import lax
from jax.experimental import pallas as pl
from jax.experimental.pallas import tpu as pltpu
from jax.sharding import PartitionSpec as P

HEADS = 12
STEP_COUNT = 6


first_decay = 0.5
second_decay = 0.5
learn_rate = 0.3
matrix_decay = 0.01
adam_epsilon = 1e-06
norm_epsilon = 1e-12
masked_score = -1000000000.0


def cut_along(value, dim, length):
    dims = value.shape
    tiles = value.reshape(*dims[:dim], length, dims[dim] // length, *dims[dim + 1 :])
    return jnp.moveaxis(tiles, dim, 0)


def sent_and_summed(value, axis, dim):
    length = lax.axis_size(axis)
    tiles = lax.all_to_all(cut_along(value, dim, length), axis, 0, 0, tiled=True)
    return jnp.sum(tiles.astype(jnp.float32), axis=0)


def layer_norm(values, gain_row, shift_row):
    center = values - jnp.mean(values, axis=-1, keepdims=True)
    spread = jnp.mean(center * center, axis=-1, keepdims=True)
    return center * lax.rsqrt(spread + norm_epsilon) * gain_row + shift_row


def norm_pair(values, gain_pair):
    return layer_norm(values, gain_pair[0], gain_pair[1])


def lamb_parts(master, moment, square, gradient, decay_rate):
    new_moment = first_decay * moment + (1.0 - first_decay) * gradient
    new_square = second_decay * square + (1.0 - second_decay) * gradient * gradient
    update = (
        new_moment
        / (1.0 - first_decay**STEP_COUNT)
        / (jnp.sqrt(new_square / (1.0 - second_decay**STEP_COUNT)) + adam_epsilon)
        + decay_rate * master
    )
    return (new_moment, new_square, update)


def gelu_tanh(values):
    return jax.nn.gelu(values, approximate=True)

MESH_ID = pl.DeviceIdType.MESH
PLANES = 4
CUT = 384


def here():
    place = lax.axis_index("dp")
    return place // 4, (place // 2) % 2, place % 2, lax.axis_index("mp")


def device_at(z, y, x, core):
    return (z * 4 + y * 2 + x, core)


def meet(peers):
    barrier = pltpu.get_barrier_semaphore()
    for peer in peers:
        pl.semaphore_signal(barrier, inc=1, device_id=peer, device_id_type=MESH_ID)
    pl.semaphore_wait(barrier, len(peers))


def chip_peers():
    z, y, x, core = here()
    peers = [device_at((z + k) % PLANES, y, x, core) for k in range(1, PLANES)]
    return peers + [device_at(z, 1 - y, x, core), device_at(z, y, 1 - x, core)]


class Gather:
    def __init__(self, held, z_send, z_recv, near_send, near_recv):
        self.held, self.z_send, self.z_recv = held, z_send, z_recv
        self.near_send, self.near_recv = near_send, near_recv

    def along_z(self, c, k):
        z, y, x, core = here()
        block = self.held.at[c, z, y, x]
        return pltpu.make_async_remote_copy(
            src_ref=block,
            dst_ref=block,
            send_sem=self.z_send.at[c, k - 1],
            recv_sem=self.z_recv.at[c, k - 1],
            device_id=device_at((z + k) % PLANES, y, x, core),
            device_id_type=MESH_ID,
        )

    def near(self, c, flip, stage):
        z, y, x, core = here()
        first_y = flip == 0
        go_y = first_y if stage == 0 else not first_y
        if stage == 0:
            block = self.held.at[c, :, y, x]
        elif go_y:
            block = self.held.at[c, :, y]
        else:
            block = self.held.at[c, :, :, x]
        target = device_at(z, 1 - y, x, core) if go_y else device_at(z, y, 1 - x, core)
        return pltpu.make_async_remote_copy(
            src_ref=block,
            dst_ref=block,
            send_sem=self.near_send.at[stage, c],
            recv_sem=self.near_recv.at[stage, c],
            device_id=target,
            device_id_type=MESH_ID,
        )

    def start_z(self, pair):
        for flip in range(2):
            for k in range(1, PLANES):
                self.along_z(2 * pair + flip, k).start()

    def start_near(self, pair, stage):
        for flip in range(2):
            self.near(2 * pair + flip, flip, stage).start()

    def wait_z(self, pair):
        for flip in range(2):
            for k in range(1, PLANES):
                self.along_z(2 * pair + flip, k).wait()

    def wait_near(self, pair, stage):
        for flip in range(2):
            self.near(2 * pair + flip, flip, stage).wait()


def gather_kernel(chunks, attention_ref, geglu_ref, held, z_send, z_recv, near_send, near_recv):
    z, y, x, _ = here()
    meet(chip_peers())
    wide = geglu_ref.shape[2] // CUT
    for c in range(chunks):
        if c < 4:
            shard = attention_ref[c]
        else:
            at = (c - 4) % wide * CUT
            shard = geglu_ref[(c - 4) // wide, :, at : at + CUT]
        held[c, z, y, x] = shard.astype(held.dtype)
    ring = Gather(held, z_send, z_recv, near_send, near_recv)
    pairs = chunks // 2
    ring.start_z(0)
    ring.start_z(1)
    ring.wait_z(0)
    ring.start_near(0, 0)

    @pl.loop(0, pairs)
    def _(pair):
        ring.wait_near(pair, 0)
        ring.start_near(pair, 1)

        @pl.when(pair + 1 < pairs)
        def _():
            ring.wait_z(pair + 1)
            ring.start_near(pair + 1, 0)

        @pl.when(pair + 2 < pairs)
        def _():
            ring.start_z(pair + 2)

        @pl.when(pair > 0)
        def _():
            ring.wait_near(pair - 1, 1)

    ring.wait_near(pairs - 1, 1)


def gather_weights(attention_master, geglu_master):
    rows = attention_master.shape[1]
    chunks = 4 + 3 * geglu_master.shape[2] // CUT
    held = pl.pallas_call(
        lambda *refs: gather_kernel(chunks, *refs),
        out_shape=jax.ShapeDtypeStruct((chunks, PLANES, 2, 2, rows, CUT), jnp.bfloat16),
        in_specs=[pl.BlockSpec(memory_space=pltpu.VMEM)] * 2,
        out_specs=pl.BlockSpec(memory_space=pltpu.VMEM),
        scratch_shapes=[
            pltpu.SemaphoreType.DMA((chunks, PLANES - 1)),
            pltpu.SemaphoreType.DMA((chunks, PLANES - 1)),
            pltpu.SemaphoreType.DMA((2, chunks)),
            pltpu.SemaphoreType.DMA((2, chunks)),
        ],
        compiler_params=pltpu.CompilerParams(
            collective_id=0, has_side_effects=True, vmem_limit_bytes=32 << 20
        ),
        name="gather_weights",
    )(attention_master, geglu_master)
    return held.reshape(chunks, rows * PLANES * 4, CUT)


class Scatter:
    def __init__(self, grads, far_got, mid_got, z_got, z_send, z_recv, near_send, near_recv):
        self.grads, self.far_got, self.mid_got, self.z_got = grads, far_got, mid_got, z_got
        self.z_send, self.z_recv = z_send, z_recv
        self.near_send, self.near_recv = near_send, near_recv

    def near(self, c, flip, stage):
        z, y, x, core = here()
        first_x = flip == 0
        go_x = first_x if stage == 0 else not first_x
        if stage == 0:
            block = self.grads.at[c, :, :, 1 - x] if go_x else self.grads.at[c, :, 1 - y]
            got = self.far_got.at[c]
        else:
            block = self.grads.at[c, :, y, 1 - x] if go_x else self.grads.at[c, :, 1 - y, x]
            got = self.mid_got.at[c]
        target = device_at(z, y, 1 - x, core) if go_x else device_at(z, 1 - y, x, core)
        return pltpu.make_async_remote_copy(
            src_ref=block,
            dst_ref=got,
            send_sem=self.near_send.at[stage, c],
            recv_sem=self.near_recv.at[stage, c],
            device_id=target,
            device_id_type=MESH_ID,
        )

    def along_z(self, c, k):
        z, y, x, core = here()
        to = (z + k) % PLANES
        return pltpu.make_async_remote_copy(
            src_ref=self.grads.at[c, to, y, x],
            dst_ref=self.z_got.at[c, k - 1],
            send_sem=self.z_send.at[c, k - 1],
            recv_sem=self.z_recv.at[c, k - 1],
            device_id=device_at(to, y, x, core),
            device_id_type=MESH_ID,
        )

    def start_near(self, pair, stage):
        for flip in range(2):
            self.near(2 * pair + flip, flip, stage).start()

    def start_z(self, pair):
        for flip in range(2):
            for k in range(1, PLANES):
                self.along_z(2 * pair + flip, k).start()

    def add_near(self, pair, stage):
        z, y, x, core = here()
        for flip in range(2):
            c = 2 * pair + flip
            self.near(c, flip, stage).wait()
            for plane in range(PLANES):
                if stage == 1:
                    mine, got = [(self.grads.at[c, plane, y, x])], [self.mid_got.at[c, plane]]
                else:
                    mine = [
                        self.grads.at[c, plane, k, x] if flip == 0 else self.grads.at[c, plane, y, k]
                        for k in range(2)
                    ]
                    got = [self.far_got.at[c, plane, k] for k in range(2)]
                for own, other in zip(mine, got):
                    own[...] = (
                        own[...].astype(jnp.float32) + other[...].astype(jnp.float32)
                    ).astype(own.dtype)

    def finish(self, pair, write):
        z, y, x, core = here()
        for flip in range(2):
            c = 2 * pair + flip
            total = self.grads[c, z, y, x].astype(jnp.float32)
            for k in range(1, PLANES):
                self.along_z(c, k).wait()
                total = total + self.z_got[c, k - 1].astype(jnp.float32)
            write(c, total)


def scatter_kernel(chunks, local_ref, out_ref, grads, far_got, mid_got, z_got, *sems):
    meet(chip_peers())
    ring = Scatter(grads, far_got, mid_got, z_got, *sems[:4])
    pairs = chunks // 2

    def fetch(pair):
        part = pl.ds(2 * pair, 2)
        return pltpu.make_async_copy(local_ref.at[part], grads.at[part], sems[4].at[pair])

    def write(c, total):
        out_ref[c] = total

    for pair in range(2):
        fetch(pair).start()
    fetch(0).wait()
    ring.start_near(0, 0)

    @pl.loop(0, pairs + 2)
    def _(pair):
        @pl.when(pair + 2 < pairs)
        def _():
            fetch(pair + 2).start()

        @pl.when(pair + 1 < pairs)
        def _():
            fetch(pair + 1).wait()
            ring.start_near(pair + 1, 0)

        @pl.when(pair < pairs)
        def _():
            ring.add_near(pair, 0)
            ring.start_near(pair, 1)

        @pl.when((pair > 0) & (pair <= pairs))
        def _():
            ring.add_near(pair - 1, 1)
            ring.start_z(pair - 1)

        @pl.when(pair > 1)
        def _():
            ring.finish(pair - 2, write)


def scatter_grads(local):
    chunks, depth, _ = local.shape
    rows = depth // (PLANES * 4)
    local = local.reshape(chunks, PLANES, 2, 2, rows, CUT)
    half = jnp.bfloat16
    return pl.pallas_call(
        lambda *refs: scatter_kernel(chunks, *refs),
        out_shape=jax.ShapeDtypeStruct((chunks, rows, CUT), jnp.float32),
        in_specs=[pl.BlockSpec(memory_space=pl.ANY)],
        out_specs=pl.BlockSpec(memory_space=pltpu.VMEM),
        scratch_shapes=[
            pltpu.VMEM((chunks, PLANES, 2, 2, rows, CUT), half),
            pltpu.VMEM((chunks, PLANES, 2, rows, CUT), half),
            pltpu.VMEM((chunks, PLANES, rows, CUT), half),
            pltpu.VMEM((chunks, PLANES - 1, rows, CUT), half),
            pltpu.SemaphoreType.DMA((chunks, PLANES - 1)),
            pltpu.SemaphoreType.DMA((chunks, PLANES - 1)),
            pltpu.SemaphoreType.DMA((2, chunks)),
            pltpu.SemaphoreType.DMA((2, chunks)),
            pltpu.SemaphoreType.DMA((chunks // 2,)),
        ],
        compiler_params=pltpu.CompilerParams(
            collective_id=1, has_side_effects=True, vmem_limit_bytes=40 << 20
        ),
        name="scatter_grads",
    )(local)


def core_sum_kernel(part_ref, out_ref, got, send, recv):
    z, y, x, core = here()
    other = device_at(z, y, x, 1 - core)
    meet([other])
    copy = pltpu.make_async_remote_copy(
        src_ref=part_ref,
        dst_ref=got,
        send_sem=send,
        recv_sem=recv,
        device_id=other,
        device_id_type=MESH_ID,
    )
    copy.start()
    copy.wait()
    out_ref[...] = (part_ref[...].astype(jnp.float32) + got[...].astype(jnp.float32)).astype(
        out_ref.dtype
    )


def core_sum(part, number):
    return pl.pallas_call(
        core_sum_kernel,
        out_shape=jax.ShapeDtypeStruct(part.shape, jnp.float32),
        in_specs=[pl.BlockSpec(memory_space=pltpu.VMEM)],
        out_specs=pl.BlockSpec(memory_space=pltpu.VMEM),
        scratch_shapes=[
            pltpu.VMEM(part.shape, part.dtype),
            pltpu.SemaphoreType.DMA,
            pltpu.SemaphoreType.DMA,
        ],
        compiler_params=pltpu.CompilerParams(collective_id=number, has_side_effects=True),
        name="core_sum_%d" % number,
    )(part)


def local(
    inputs,
    cotangent,
    lengths,
    masked,
    replace_ids,
    attention_master,
    attention_moment,
    attention_square,
    geglu_master,
    geglu_moment,
    geglu_square,
    embed_master,
    embed_moment,
    embed_square,
    norms_master,
    norms_moment,
    norms_square,
):
    half_type = jnp.bfloat16
    full_type = jnp.float32
    tokens_here = inputs.shape[0]
    width = inputs.shape[1]
    head_dim = width // HEADS
    local_heads = HEADS // lax.axis_size("mp")
    block_len = min(tokens_here, 512)
    attn_scale = 1.0 / math.sqrt(head_dim)
    column_count = embed_master.shape[1]
    owners = lax.axis_size("dp")
    own_comm = owners == 16 and attention_master.shape[1:] == (48, CUT)
    if own_comm:
        held = gather_weights(attention_master, geglu_master)
        attn_low = held[:4]
        wide = geglu_master.shape[2] // CUT
        geglu_low = jnp.concatenate([held[4 + k :: wide] for k in range(wide)], axis=2)
    else:
        attn_low, geglu_low = (
            lax.all_gather(attention_master.astype(half_type), "dp", axis=1, tiled=True),
            lax.all_gather(geglu_master.astype(half_type), "dp", axis=1, tiled=True),
        )

    def mp_sum(value, number):
        if own_comm:
            return core_sum(value, number)
        return lax.psum(value, "mp").astype(full_type)

    owner_rows = embed_master.shape[0]
    per_owner = tokens_here // owners
    owner_low = jnp.arange(owners, dtype=jnp.int32)[:, None] * owner_rows
    owned = (replace_ids[None, :] >= owner_low) & (replace_ids[None, :] < owner_low + owner_rows)
    order = jnp.arange(tokens_here, dtype=jnp.int32)
    earlier = (order[:, None] < order[None, :]).astype(half_type)
    rank = jnp.dot(owned.astype(half_type), earlier, preferred_element_type=full_type)
    owner_at = jnp.arange(owners, dtype=full_type)[:, None] * per_owner
    target = jnp.sum(jnp.where(owned, rank + owner_at, 0.0), axis=0).astype(jnp.int32)
    moves = target[None, :] == order[:, None]
    sorted_ids = jnp.sum(jnp.where(moves, replace_ids[None, :], 0), axis=1)
    asked = lax.all_to_all(sorted_ids, "dp", 0, 0, tiled=True)
    asked = asked - lax.axis_index("dp") * owner_rows
    hits = asked[:, None] == jnp.arange(owner_rows, dtype=jnp.int32)[None, :]
    sent_rows = jnp.dot(
        hits.astype(half_type), embed_master.astype(half_type), preferred_element_type=full_type
    ).astype(half_type)
    got_rows = lax.all_to_all(sent_rows, "dp", 0, 0, tiled=True)
    looked_cols = jnp.einsum(
        "pt,pc->tc", moves.astype(half_type), got_rows, preferred_element_type=full_type
    ).astype(half_type)
    looked = lax.all_gather(looked_cols, "mp", axis=1, tiled=True)
    is_masked = masked[:, None] == 1
    hidden_in = jnp.where(is_masked, looked.astype(full_type), inputs.astype(full_type))
    length_row = lengths[0]
    places = jnp.arange(tokens_here, dtype=jnp.int32)
    ends_at = jnp.cumsum(length_row)
    segment_ids = jnp.sum((ends_at[None, :] <= places[:, None]).astype(jnp.int32), axis=1)
    live_rows = (places < jnp.sum(length_row)).astype(full_type)[:, None]
    token_count = jnp.sum(length_row).astype(full_type)
    head_ids = lax.axis_index("mp") * local_heads + jnp.arange(local_heads, dtype=jnp.int32)
    slopes = 2.0 ** (-8.0 * (head_ids.astype(full_type) + 1.0) / HEADS)
    act_low = hidden_in.astype(half_type)
    qkv_low = jnp.einsum(
        "td,kdc->ktc", act_low, attn_low[:3], preferred_element_type=full_type
    ).astype(half_type)
    head_vals = qkv_low.reshape(3, tokens_here, local_heads, head_dim)

    def block_scores(begin_at, query_blk):
        query_pos = begin_at + jnp.arange(block_len, dtype=jnp.int32)
        scores = (
            jnp.einsum("qhe,khe->hqk", query_blk, head_vals[1], preferred_element_type=full_type)
            * attn_scale
        )
        distance = jnp.abs(query_pos[:, None] - places[None, :]).astype(full_type)
        scores = scores - slopes[:, None, None] * distance[None]
        same_seq = segment_ids[:, None] == segment_ids[None, :]
        return jnp.where(same_seq[None], scores, masked_score)

    def forward_block(begin_at):
        query_blk = head_vals[0]
        scores = block_scores(begin_at, query_blk)
        top_score = jnp.max(scores, axis=-1, keepdims=True)
        raised = jnp.exp(scores - top_score)
        row_total = jnp.sum(raised, axis=-1, keepdims=True)
        weights = (raised / row_total).astype(half_type)
        context_blk = jnp.einsum(
            "hqk,khe->qhe", weights, head_vals[2], preferred_element_type=full_type
        )
        return (context_blk.astype(half_type), (top_score + jnp.log(row_total))[..., 0])

    starts = jnp.arange(tokens_here // block_len, dtype=jnp.int32) * block_len
    context_blocks, lse_blocks = lax.map(forward_block, starts)
    context = context_blocks.reshape(tokens_here, local_heads * head_dim)
    attn_part = jnp.einsum("tc,dc->td", context, attn_low[3], preferred_element_type=full_type)
    attn_out = mp_sum(attn_part, 2)
    normed_one, first_back = jax.vjp(norm_pair, hidden_in + attn_out, norms_master[0:2])
    normed_low = normed_one.astype(half_type)
    gate_up = jnp.einsum("td,kdf->ktf", normed_low, geglu_low[:2], preferred_element_type=full_type)
    gelu_val, gelu_back = jax.vjp(gelu_tanh, gate_up[0])
    inner_act = (gelu_val * gate_up[1]).astype(half_type)
    geglu_part = jnp.einsum("tf,df->td", inner_act, geglu_low[2], preferred_element_type=full_type)
    geglu_out = mp_sum(geglu_part, 2)
    result, second_back = jax.vjp(norm_pair, normed_one + geglu_out, norms_master[2:4])
    squares = jnp.stack(
        [
            jnp.sum(hidden_in * hidden_in * live_rows),
            jnp.sum(attn_out * attn_out * live_rows),
            jnp.sum(geglu_out * geglu_out * live_rows),
        ]
    )
    count_total, square_total = lax.psum((token_count, squares), "dp")
    rms_stats = jnp.sqrt(square_total / (count_total * width) + 1e-06)
    grad_second, norm_grad_two = second_back(cotangent.astype(full_type) * live_rows)
    grad_geglu = grad_second.astype(half_type)
    grad_inner = jnp.einsum("td,df->tf", grad_geglu, geglu_low[2], preferred_element_type=full_type)
    down_grad = jnp.einsum("td,tf->df", grad_geglu, inner_act, preferred_element_type=full_type)
    grad_gate = gelu_back(grad_inner * gate_up[1])[0]
    grad_up = grad_inner * gelu_val
    grad_gu = jnp.stack([grad_gate, grad_up]).astype(half_type)
    gu_grad = jnp.einsum("td,ktf->kdf", normed_low, grad_gu, preferred_element_type=full_type)
    geglu_local = jnp.concatenate([gu_grad, down_grad[None]], axis=0)
    back_part = jnp.einsum("ktf,kdf->td", grad_gu, geglu_low[:2], preferred_element_type=full_type)
    grad_normed = grad_second + mp_sum(back_part, 2)
    grad_first_in, norm_grad_one = first_back(grad_normed)
    grad_attn = grad_first_in.astype(half_type)
    grad_context = jnp.einsum(
        "td,dc->tc", grad_attn, attn_low[3], preferred_element_type=full_type
    ).astype(half_type)
    out_grad = jnp.einsum("td,tc->dc", grad_attn, context, preferred_element_type=full_type)
    grad_heads = grad_context.reshape(tokens_here, local_heads, head_dim)

    def backward_block(carry, packed):
        key_acc, value_acc = carry
        begin_at, lse_blk = packed
        query_blk = head_vals[0]
        scores = block_scores(begin_at, query_blk)
        weights = jnp.exp(scores - lse_blk[..., None])
        grad_weights = jnp.einsum(
            "qhe,khe->hqk", grad_heads, head_vals[2], preferred_element_type=full_type
        )
        value_acc = value_acc + jnp.einsum(
            "hqk,qhe->khe", weights.astype(half_type), grad_heads, preferred_element_type=full_type
        )
        row_inner = jnp.sum(grad_weights * weights, axis=-1, keepdims=True)
        grad_scores = (weights * (grad_weights - row_inner)).astype(half_type)
        grad_query = (
            jnp.einsum("hqk,khe->qhe", grad_scores, head_vals[1], preferred_element_type=full_type)
            * attn_scale
        )
        key_acc = (
            key_acc
            + jnp.einsum("hqk,qhe->khe", grad_scores, query_blk, preferred_element_type=full_type)
            * attn_scale
        )
        return ((key_acc, value_acc), grad_query.astype(half_type))

    zero_heads = jnp.zeros((tokens_here, local_heads, head_dim), full_type)
    (key_acc, value_acc), query_grads = lax.scan(
        backward_block, (zero_heads, zero_heads), (starts, lse_blocks)
    )
    grad_qkv = jnp.stack(
        [
            query_grads.reshape(tokens_here, -1),
            key_acc.reshape(tokens_here, -1).astype(half_type),
            value_acc.reshape(tokens_here, -1).astype(half_type),
        ]
    )
    qkv_grad = jnp.einsum("td,ktc->kdc", act_low, grad_qkv, preferred_element_type=full_type)
    act_part = jnp.einsum("ktc,kdc->td", grad_qkv, attn_low[:3], preferred_element_type=full_type)
    grad_in = grad_first_in + mp_sum(act_part.astype(jnp.bfloat16), 3)
    input_grad = jnp.where(is_masked, 0.0, grad_in)
    attention_local = jnp.concatenate([qkv_grad, out_grad[None]], axis=0)
    own_columns = lax.dynamic_slice_in_dim(
        grad_in, lax.axis_index("mp") * column_count, column_count, 1
    )
    picked = jnp.where(is_masked, own_columns, 0.0)
    highest = lax.Precision.HIGHEST
    sorted_grads = jnp.dot(moves.astype(full_type), picked, precision=highest)
    got_grads = lax.all_to_all(sorted_grads, "dp", 0, 0, tiled=True)
    embed_summed = jnp.einsum("pr,pc->rc", hits.astype(full_type), got_grads, precision=highest)
    if own_comm:
        geglu_cut = geglu_local.astype(half_type).reshape(3, width, wide, CUT)
        geglu_cut = jnp.moveaxis(geglu_cut, 2, 1).reshape(3 * wide, width, CUT)
        summed = scatter_grads(
            jnp.concatenate([attention_local.astype(half_type), geglu_cut], axis=0)
        )
        attention_summed = summed[:4]
        geglu_summed = jnp.concatenate([summed[4 + k :: wide] for k in range(wide)], axis=2)
    else:
        attention_summed, geglu_summed = (
            sent_and_summed(attention_local.astype(jnp.bfloat16), "dp", 1),
            sent_and_summed(geglu_local.astype(jnp.bfloat16), "dp", 1),
        )
    inverse_count = 1.0 / count_total
    attention_grad = attention_summed * inverse_count
    geglu_grad = geglu_summed * inverse_count
    embed_grad = embed_summed * inverse_count
    attention_first, attention_second, attention_update = lamb_parts(
        attention_master, attention_moment, attention_square, attention_grad, matrix_decay
    )
    geglu_first, geglu_second, geglu_update = lamb_parts(
        geglu_master, geglu_moment, geglu_square, geglu_grad, matrix_decay
    )
    embed_first, embed_second, embed_update = lamb_parts(
        embed_master, embed_moment, embed_square, embed_grad, matrix_decay
    )
    weight_squares = jnp.concatenate(
        [
            jnp.sum(attention_master * attention_master, axis=(1, 2)),
            jnp.sum(geglu_master * geglu_master, axis=(1, 2)),
            jnp.sum(embed_master * embed_master)[None],
        ]
    )
    update_squares = jnp.concatenate(
        [
            jnp.sum(attention_update * attention_update, axis=(1, 2)),
            jnp.sum(geglu_update * geglu_update, axis=(1, 2)),
            jnp.sum(embed_update * embed_update)[None],
        ]
    )
    norms_local = jnp.concatenate([norm_grad_one, norm_grad_two], axis=0)
    weight_total, update_total, norms_summed = lax.psum(
        (weight_squares, update_squares, norms_local * 0.5), ("dp", "mp")
    )
    weight_norms = jnp.sqrt(weight_total)
    update_norms = jnp.sqrt(update_total)
    ratios = weight_norms / update_norms
    attention_new = attention_master - learn_rate * ratios[0:4][:, None, None] * attention_update
    geglu_new = geglu_master - learn_rate * ratios[4:7][:, None, None] * geglu_update
    embed_new = embed_master - learn_rate * ratios[7] * embed_update
    norms_grad = norms_summed * inverse_count
    norms_first, norms_second, norms_update = lamb_parts(
        norms_master, norms_moment, norms_square, norms_grad, 0.0
    )
    norm_weight = jnp.sqrt(jnp.sum(norms_master * norms_master, axis=1))
    norm_update = jnp.sqrt(jnp.sum(norms_update * norms_update, axis=1))
    norms_new = norms_master - learn_rate * (norm_weight / norm_update)[:, None] * norms_update
    lamb_norms = jnp.stack(
        [jnp.concatenate([weight_norms, norm_weight]), jnp.concatenate([update_norms, norm_update])]
    )
    return (
        result,
        input_grad,
        rms_stats,
        lamb_norms,
        attention_grad,
        attention_first,
        attention_second,
        attention_new,
        geglu_grad,
        geglu_first,
        geglu_second,
        geglu_new,
        embed_grad,
        embed_first,
        embed_second,
        embed_new,
        norms_grad,
        norms_first,
        norms_second,
        norms_new,
    )


def solution(mesh):
    in_specs = (
        P("dp", None),
        P("dp", None),
        P("dp", None),
        P("dp"),
        P("dp"),
        P(None, "dp", "mp"),
        P(None, "dp", "mp"),
        P(None, "dp", "mp"),
        P(None, "dp", "mp"),
        P(None, "dp", "mp"),
        P(None, "dp", "mp"),
        P("dp", "mp"),
        P("dp", "mp"),
        P("dp", "mp"),
        P(),
        P(),
        P(),
    )
    out_specs = (
        P("dp", None),
        P("dp", None),
        P(),
        P(),
        P(None, "dp", "mp"),
        P(None, "dp", "mp"),
        P(None, "dp", "mp"),
        P(None, "dp", "mp"),
        P(None, "dp", "mp"),
        P(None, "dp", "mp"),
        P(None, "dp", "mp"),
        P(None, "dp", "mp"),
        P("dp", "mp"),
        P("dp", "mp"),
        P("dp", "mp"),
        P("dp", "mp"),
        P(),
        P(),
        P(),
        P(),
    )
    return jax.shard_map(local, mesh=mesh, in_specs=in_specs, out_specs=out_specs, check_vma=False)
```
